128 devices in a mesh: grp: 4 (over z), dev: 32 (over x, y, core).
Axes of the slice: x: 4, y: 4, z: 4, core: 2. Of those that a mesh axis runs over, the one named last changes fastest.
Arguments:
- trace: bfloat16 [786432, 256], P(('grp', 'dev')), may hold values from -6 to 6
- counts: int32 [4, 32, 32], P('grp', 'dev'), may hold values from 1 to 192, as said below
Outputs:
- cross_corr: float32 [256, 128, 128], P(('grp', 'dev'))
The draws below stay inside these ranges and needn't reach their ends.
Inputs may be any that keep to these rules, and one draw needn't show every extreme that they name: Every destination column counts[g, :, d] sums to 3072, and in every column one entry equals 192.
All inputs are finite; a program needn't handle non-finite values.
Results may differ from the reference program's by a relative error of at most 0.0003.
Values may be sent and summed in bfloat16 or wider, within the bound.
A program may use at most 128 MiB of HBM per device.

```python
import math
import jax
import jax.numpy as jnp
from jax import lax

NU = 128
LAGS = 256
TRACE_DEV = 3072
GROUPS = 4
DEVS = 32
SLOT = 192
CAP = 6144
CH = 256


def draw_counts(key, part):
    half_slot = SLOT // 2
    first_key, second_key = jax.random.split(key)
    spread = jax.random.randint(first_key, (GROUPS, DEVS, DEVS), 1, half_slot)
    peak = jax.random.randint(second_key, (GROUPS, DEVS, 1), 0, DEVS)
    source = jnp.arange(DEVS, dtype=jnp.int32)[None, None, :]
    spread = jnp.where(source == peak, half_slot, spread)
    spread = jnp.where(source == (peak + 1) % DEVS, 0, spread)
    column = half_slot + spread - jnp.roll(spread, -1, axis=2)
    return jnp.transpose(column, (0, 2, 1)).astype(jnp.int32)


def block_levels(key, shape, cuts, smallest, high):
    loudness = 1.0
    for axis_at, blocks in cuts:
        draws = jax.random.uniform(jax.random.fold_in(jax.random.fold_in(key, 6), axis_at), (blocks,), jnp.float32, smallest / len(cuts), high / len(cuts))
        loudness = loudness * jnp.repeat(jnp.exp(draws), shape[axis_at] // blocks).reshape((-1,) + (1,) * (len(shape) - 1 - axis_at))
    return loudness


def bell_draw(rng, shape, deviation, bound, cuts=(), kind=jnp.bfloat16):
    loudness = block_levels(rng, shape, cuts, -0.22, 0.18) if cuts else 1.0
    drawn = jax.random.normal(rng, shape, jnp.float32) * deviation * loudness
    return jnp.minimum(jnp.maximum(drawn, -bound), bound).astype(kind)


def setup_inputs(seed: int = 0) -> dict:
    splits = jax.random.split(jax.random.key(seed), 3)
    return {
        "trace": bell_draw(splits[0], (GROUPS * DEVS * CAP, CH), 1.0, 6.0, ((0, 128),)),
        "counts": draw_counts(jax.random.fold_in(splits[2], 71), 0),
    }


def reference(trace, counts):
    starts = jnp.cumsum(counts, axis=2) - counts
    offsets = jnp.cumsum(counts, axis=1) - counts
    start_t = jnp.transpose(starts, (0, 2, 1))
    offset_t = jnp.transpose(offsets, (0, 2, 1))
    row_ids = jnp.arange(TRACE_DEV, dtype=jnp.int32)
    before = (offset_t[:, :, None, :] <= row_ids[None, None, :, None]).astype(jnp.int32)
    source = lax.optimization_barrier(jnp.sum(before, axis=3)) - 1
    onehot = jnp.arange(DEVS, dtype=jnp.int32)[None, None, None, :] == source[..., None]
    shift_rows = lax.optimization_barrier(jnp.sum(jnp.where(onehot, (start_t - offset_t)[:, :, None, :], 0), axis=3))
    group_ids = jnp.arange(GROUPS, dtype=jnp.int32)[:, None, None]
    flat_index = ((group_ids * DEVS + source) * CAP + shift_rows + row_ids[None, None, :]).astype(jnp.int32)
    stream = trace[flat_index.reshape(-1)].reshape(GROUPS, DEVS * TRACE_DEV, CH)
    sensor = stream[:, :, NU:].astype(jnp.float32)
    power_rows = jnp.concatenate([jnp.zeros((GROUPS, LAGS, NU), jnp.float32), stream[:, :, :NU].astype(jnp.float32)], axis=1)
    norm_scale = 1.0 / math.sqrt(GROUPS * DEVS * TRACE_DEV)

    def one_lag(lag_index):
        shifted = lax.dynamic_slice_in_dim(power_rows, (LAGS - lag_index).astype(jnp.int32), DEVS * TRACE_DEV, axis=1)
        return jnp.einsum('gti,gtc->ic', sensor, shifted, precision=lax.Precision.HIGHEST) * norm_scale
    return lax.map(one_lag, jnp.arange(LAGS, dtype=jnp.int32))
```

```python
import functools
import math

import jax
import jax.numpy as jnp
from jax import lax
from jax.experimental import pallas as pl
from jax.experimental.pallas import tpu as pltpu
from jax.sharding import PartitionSpec as P

NU = 128
LAGS = 256
MESH = pl.DeviceIdType.MESH
DIMS = 6
BLOCKS = 64
HALO = 256
LEAD = 240
PARTS = (48, 40, 40, 48, 40, 40)
PART_AT = (0, 48, 88, 128, 176, 216)
K_CHUNK = 2048


def pack_kernel(per_step, slot, counts_ref, trace_ref, out_ref, rows_ref):
    step = pl.program_id(0)
    capacity = trace_ref.shape[0]
    top = capacity - slot - 16

    def skip(d, total):
        return total + counts_ref[d]

    start = lax.fori_loop(0, step * per_step, skip, jnp.int32(0))
    for i in range(per_step):
        base = pl.multiple_of(jnp.minimum(start // 16 * 16, top), 16)
        for j in range(2):
            half = slice(j * NU, (j + 1) * NU)
            rows_ref[i, j] = trace_ref[pl.ds(base, slot + 16), half].astype(jnp.float32)
            out_ref[i, :, half] = rows_ref[i, j, pl.ds(start - base, slot), :].astype(out_ref.dtype)
        start = start + counts_ref[step * per_step + i]


def pack(counts, trace, slots, slot):
    per_step = 4
    return pl.pallas_call(
        functools.partial(pack_kernel, per_step, slot),
        out_shape=jax.ShapeDtypeStruct((slots, slot, trace.shape[1]), trace.dtype),
        grid_spec=pltpu.PrefetchScalarGridSpec(
            num_scalar_prefetch=1,
            grid=(slots // per_step,),
            in_specs=[pl.BlockSpec(trace.shape, lambda i, c: (0, 0))],
            out_specs=pl.BlockSpec((per_step, slot, trace.shape[1]), lambda i, c: (i, 0, 0)),
            scratch_shapes=[pltpu.VMEM((per_step, 2, slot + 16, NU), jnp.float32)],
        ),
        name="pack_rows",
    )(counts, trace)


def unpack_kernel(per_step, counts_ref, recv_ref, sensor_ref, power_ref, rows_ref):
    step = pl.program_id(0)
    slot = recv_ref.shape[1]
    owned = power_ref.shape[0]

    def skip(s, total):
        return total + counts_ref[s]

    at = lax.fori_loop(0, step * per_step, skip, jnp.int32(0))
    for i in range(per_step):
        for j in range(2):
            half = recv_ref[i, :, j * NU:(j + 1) * NU]
            rows_ref[j, pl.ds(at, slot), :] = half.astype(jnp.float32)
        at = at + counts_ref[step * per_step + i]

    @pl.when(step == pl.num_programs(0) - 1)
    def _():
        def tile(k, carry):
            here = pl.multiple_of(k * 128, 128)
            power_ref[pl.ds(here, 128), :] = rows_ref[0, pl.ds(here, 128), :].astype(power_ref.dtype)
            block = rows_ref[1, pl.ds(here, 128), :]
            sensor_ref[:, pl.ds(here, 128)] = block.T.astype(sensor_ref.dtype)
            return carry

        lax.fori_loop(0, owned // 128, tile, 0)


def unpack(counts, recv, owned):
    per_step = 4
    slots, slot, width = recv.shape
    return pl.pallas_call(
        functools.partial(unpack_kernel, per_step),
        out_shape=(
            jax.ShapeDtypeStruct((NU, owned), recv.dtype),
            jax.ShapeDtypeStruct((owned, NU), recv.dtype),
        ),
        grid_spec=pltpu.PrefetchScalarGridSpec(
            num_scalar_prefetch=1,
            grid=(slots // per_step,),
            in_specs=[pl.BlockSpec((per_step, slot, width), lambda i, c: (i, 0, 0))],
            out_specs=(
                pl.BlockSpec((NU, owned), lambda i, c: (0, 0)),
                pl.BlockSpec((owned, NU), lambda i, c: (0, 0)),
            ),
            scratch_shapes=[pltpu.VMEM((2, owned + slot, NU), jnp.float32)],
        ),
        name="unpack_rows",
    )(counts, recv)


def corr_kernel(scale, sensor_ref, power_ref, out_ref, *scratch):
    (wide, landed, rows, shifted, head, ex_send, ex_recv, edge_send, edge_recv,
     rs_send, rs_recv) = scratch[:11]
    acc = scratch[11:17]
    got = scratch[17:23]
    owned = power_ref.shape[0]
    total = 2 * owned
    grp = lax.axis_index("grp")
    dev = lax.axis_index("dev")
    core = dev % 2
    chip = dev // 2
    y = chip % 4
    x = chip // 4
    partner = (grp, dev + 1 - 2 * core)
    after = (chip + 1) % 16
    before = (chip + 15) % 16

    def place(xx, yy, zz):
        return (zz, xx * 8 + yy * 2 + core)

    def near(a):
        return a + 1 - 2 * (a % 2)

    def far(a):
        return 3 - a

    neighbours = (
        place(near(x), y, grp), place(x, near(y), grp), place(x, y, near(grp)),
        place(far(x), y, grp), place(x, far(y), grp), place(x, y, far(grp)),
    )

    def near_bit(a):
        return (a // 2 + a % 2) % 2

    own_bits = (near_bit(x), near_bit(y), near_bit(grp), x // 2, y // 2, grp // 2)

    barrier = pltpu.get_barrier_semaphore()

    def greet(target):
        pl.semaphore_signal(barrier, inc=1, device_id=target, device_id_type=MESH)

    greet(partner)
    for target in neighbours:
        greet(target)
    greet((grp, before * 2 + 1))
    greet((grp, after * 2))
    greet((grp, jnp.where(core == 1, after * 2 + 1, before * 2)))
    pl.semaphore_wait(barrier, 10)

    own_at = pl.multiple_of(core * owned, 128)
    here = (
        (sensor_ref, wide.at[0:NU, pl.ds(own_at, owned)]),
        (power_ref, landed.at[pl.ds(pl.multiple_of(HALO + core * owned, 128), owned), :]),
    )
    exchange = [
        pltpu.make_async_remote_copy(
            src_ref=src, dst_ref=dst, send_sem=ex_send.at[i], recv_sem=ex_recv.at[i],
            device_id=partner, device_id_type=MESH)
        for i, (src, dst) in enumerate(here)
    ]
    edges = (
        (sensor_ref.at[:, 0:128], head, before),
        (power_ref.at[pl.ds(owned - HALO, HALO), :], landed.at[0:HALO, :], after),
    )

    def edge_copy(i, which):
        src, dst, target = edges[i]
        return pltpu.make_async_remote_copy(
            src_ref=src, dst_ref=dst, send_sem=edge_send.at[which], recv_sem=edge_recv.at[i],
            device_id=(grp, target * 2 + which), device_id_type=MESH)

    for i in range(2):
        @pl.when(core == i)
        def _(i=i):
            for which in range(2):
                edge_copy(i, which).start()

    for copy in exchange:
        copy.start()
    wide[0:NU, pl.ds(own_at, owned)] = sensor_ref[...]
    power_at = pl.multiple_of(HALO + core * owned, 128)
    rows[pl.ds(power_at, owned), :] = power_ref[...].astype(jnp.float32)
    exchange[1].wait_recv()
    other_at = pl.multiple_of(HALO + (1 - core) * owned, 128)
    rows[pl.ds(other_at, owned), :] = landed[pl.ds(other_at, owned), :].astype(jnp.float32)
    edge_copy(1, 0).wait_recv()
    rows[0:HALO, :] = jnp.where(chip > 0, landed[0:HALO, :].astype(jnp.float32), 0.0)

    def shift_rows(k, carry):
        at = pl.multiple_of(k * 912, 16)
        for u in range(4):
            shifted[u, pl.ds(at, 912), :] = rows[
                pl.ds(at + 16 - 4 * u - 2 * core, 912), :].astype(shifted.dtype)
        return carry

    lax.fori_loop(0, (LEAD + total) // 912, shift_rows, 0)

    edge_copy(0, 0).wait_recv()
    exchange[0].wait_recv()
    lane = lax.broadcasted_iota(jnp.int32, (NU, 128), 1)

    def turn(block):
        return pltpu.roll(block.astype(jnp.float32), 127, 1)

    def shift_lanes(k, following):
        at = pl.multiple_of(total - 128 - k * 128, 128)
        turned = turn(wide[0:NU, pl.ds(at, 128)])
        wide[NU:2 * NU, pl.ds(at, 128)] = jnp.where(lane == 127, following, turned).astype(wide.dtype)
        return turned

    lax.fori_loop(0, total // 128, shift_lanes, jnp.where(chip < 15, turn(head[...]), 0.0))

    def step_copy(step, q, src, dst):
        return pltpu.make_async_remote_copy(
            src_ref=src, dst_ref=dst, send_sem=rs_send.at[step, q], recv_sem=rs_recv.at[step, q],
            device_id=neighbours[(q + step) % DIMS], device_id_type=MESH)

    def read_at(bits):
        flip = [(o + b) % 2 for o, b in zip(own_bits, bits)]
        xd, yd, zd = (2 * flip[3 + i] + (flip[i] + flip[3 + i]) % 2 for i in range(3))
        return yd, pl.multiple_of(LEAD - 16 * (zd * 4 + xd), 16)

    def pair(i, carry):
        first = BLOCKS - 1 - 2 * i
        both = []
        for block in (first, first - 1):
            bits = [(block // 2 ** b) % 2 for b in range(DIMS)]
            both.append((bits, read_at(bits)))
        result = None
        for k in range(0, total, K_CHUNK):
            operand = jnp.concatenate(
                [shifted[u, pl.ds(at + k, K_CHUNK), :] for _, (u, at) in both], axis=1)
            term = jnp.dot(wide[:, k:k + K_CHUNK], operand, preferred_element_type=jnp.float32)
            result = term if result is None else result + term
        for j, (bits, _) in enumerate(both):
            for q in range(DIMS):
                index = sum(bits[(q + e) % DIMS] * 2 ** (DIMS - 1 - e) for e in range(DIMS))
                acc[q][index] = result[PART_AT[q]:PART_AT[q] + PARTS[q], j * NU:(j + 1) * NU]

                @pl.when(bits[q] == 1)
                def _(q=q, index=index):
                    step_copy(0, q, acc[q].at[index], got[q].at[index - BLOCKS // 2]).start()
        return carry

    lax.fori_loop(0, BLOCKS // 2, pair, 0)

    sent = [[step_copy(0, q, acc[q].at[32:64], got[q].at[0:32]) for q in range(DIMS)]]
    begin = 0
    for step in range(1, DIMS):
        n = 2 ** (DIMS - 1 - step)
        copies = []
        for q in range(DIMS):
            sent[step - 1][q].wait_recv()
            acc[q][n:2 * n] = acc[q][n:2 * n] + got[q][begin + n:begin + 2 * n]
            copy = step_copy(
                step, q, acc[q].at[n:2 * n], got[q].at[begin + 2 * n:begin + 3 * n])
            copy.start()
            copies.append(copy)
        for q in range(DIMS):
            acc[q][0:n] = acc[q][0:n] + got[q][begin:begin + n]
        sent.append(copies)
        begin += 2 * n
    for q in range(DIMS):
        sent[DIMS - 1][q].wait_recv()
        out_ref[PART_AT[q]:PART_AT[q] + PARTS[q], :] = (acc[q][0] + got[q][begin]) * scale

    for copies in sent:
        for copy in copies:
            copy.wait_send()
    for copy in exchange:
        copy.wait_send()

    for i in range(2):
        @pl.when(core == i)
        def _(i=i):
            for which in range(2):
                edge_copy(i, which).wait_send()


def correlate(sensor, power, scale):
    owned = power.shape[0]
    total = 2 * owned
    kind = power.dtype
    return pl.pallas_call(
        functools.partial(corr_kernel, scale),
        out_shape=jax.ShapeDtypeStruct((2 * NU, NU), jnp.float32),
        in_specs=[pl.BlockSpec(memory_space=pltpu.VMEM)] * 2,
        out_specs=pl.BlockSpec(memory_space=pltpu.VMEM),
        scratch_shapes=[
            pltpu.VMEM((2 * NU, total), kind),
            pltpu.VMEM((HALO + total, NU), kind),
            pltpu.VMEM((HALO + total, NU), jnp.float32),
            pltpu.VMEM((4, LEAD + total, NU), kind),
            pltpu.VMEM((NU, 128), kind),
            pltpu.SemaphoreType.DMA((2,)),
            pltpu.SemaphoreType.DMA((2,)),
            pltpu.SemaphoreType.DMA((2,)),
            pltpu.SemaphoreType.DMA((2,)),
            pltpu.SemaphoreType.DMA((DIMS, DIMS)),
            pltpu.SemaphoreType.DMA((DIMS, DIMS)),
        ]
        + [pltpu.VMEM((BLOCKS, h, NU), jnp.float32) for h in PARTS]
        + [pltpu.VMEM((BLOCKS - 1, h, NU), jnp.float32) for h in PARTS],
        compiler_params=pltpu.CompilerParams(
            collective_id=0, has_side_effects=True, vmem_limit_bytes=56 << 20),
        name="correlate_scatter",
    )(sensor, power)


def per_device(trace, counts):
    dev_count = lax.axis_size("dev")
    group_count = lax.axis_size("grp")
    capacity = trace.shape[0]
    slot_rows = capacity // dev_count
    owned = capacity // 2
    send_counts = counts.reshape(-1)
    recv_counts = lax.all_to_all(
        send_counts.reshape(dev_count, 1), "dev", split_axis=0, concat_axis=0, tiled=True
    ).reshape(-1)
    packed = pack(send_counts, trace, dev_count, slot_rows)
    received = lax.all_to_all(packed, "dev", split_axis=0, concat_axis=0, tiled=True)
    sensor, power = unpack(recv_counts, received, owned)
    scale = 1.0 / math.sqrt(group_count * dev_count * owned)
    return correlate(sensor, power, scale).reshape(2, NU, NU)


def solution(mesh):
    in_specs = (P(("grp", "dev"), None), P("grp", "dev", None))
    out_specs = P(("grp", "dev"), None, None)
    return jax.shard_map(
        per_device, mesh=mesh, in_specs=in_specs, out_specs=out_specs, check_vma=False
    )
```

```python
import functools
import math

import jax
import jax.numpy as jnp
from jax import lax
from jax.experimental import pallas as pl
from jax.experimental.pallas import tpu as pltpu
from jax.sharding import PartitionSpec as P

NU = 128
LAGS = 256
MESH = pl.DeviceIdType.MESH
DIMS = 6
BLOCKS = 64
HALO = 256
LEAD = 240
PARTS = (48, 40, 40, 48, 40, 40)
PART_AT = (0, 48, 88, 128, 176, 216)
K_CHUNK = 2048


def pack_kernel(per_step, slot, counts_ref, trace_ref, out_ref, rows_ref):
    step = pl.program_id(0)
    capacity = trace_ref.shape[0]
    top = capacity - slot - 16

    def skip(d, total):
        return total + counts_ref[d]

    start = lax.fori_loop(0, step * per_step, skip, jnp.int32(0))
    for i in range(per_step):
        base = pl.multiple_of(jnp.minimum(start // 16 * 16, top), 16)
        for j in range(2):
            half = slice(j * NU, (j + 1) * NU)
            rows_ref[i, j] = trace_ref[pl.ds(base, slot + 16), half].astype(jnp.float32)
            out_ref[i, :, half] = rows_ref[i, j, pl.ds(start - base, slot), :].astype(out_ref.dtype)
        start = start + counts_ref[step * per_step + i]


def pack(counts, trace, slots, slot):
    per_step = 4
    return pl.pallas_call(
        functools.partial(pack_kernel, per_step, slot),
        out_shape=jax.ShapeDtypeStruct((slots, slot, trace.shape[1]), trace.dtype),
        grid_spec=pltpu.PrefetchScalarGridSpec(
            num_scalar_prefetch=1,
            grid=(slots // per_step,),
            in_specs=[pl.BlockSpec(trace.shape, lambda i, c: (0, 0))],
            out_specs=pl.BlockSpec((per_step, slot, trace.shape[1]), lambda i, c: (i, 0, 0)),
            scratch_shapes=[pltpu.VMEM((per_step, 2, slot + 16, NU), jnp.float32)],
        ),
        name="pack_rows",
    )(counts, trace)


def exchange_kernel(lengths_ref, packed_ref, recv_ref, table_ref, mid, turn_first, turn_last,
                    table_send, table_recv, send_sem, recv_sem, own_sem):
    slots = table_ref.shape[0]
    grp = lax.axis_index("grp")
    dev = lax.axis_index("dev")
    core = dev % 2
    y = dev // 2 % 4
    x = dev // 8
    barrier = pltpu.get_barrier_semaphore()

    def greet(k, carry):
        pl.semaphore_signal(barrier, inc=1, device_id=(grp, (dev + k) % slots), device_id_type=MESH)
        return carry

    lax.fori_loop(1, slots, greet, 0)
    used = []

    def remote(src, dst, target):
        i = len(used)
        copy = pltpu.make_async_remote_copy(
            src_ref=src, dst_ref=dst, send_sem=send_sem.at[i], recv_sem=recv_sem.at[i],
            device_id=(grp, target), device_id_type=MESH)
        used.append(copy)
        return copy

    def cell(ref, h, a, b, c):
        return ref.at[a, b, c, h] if h == 0 else ref.at[b, a, c, h]

    def block(h, a, c=slice(None)):
        return packed_ref.at[a, :, c, h] if h == 0 else packed_ref.at[:, a, c, h]

    at = ((x, y), (y, x))

    def place(h, da, db, dc):
        a = (at[h][0] + da) % 4
        b = (at[h][1] + db) % 4
        c = (core + dc) % 2
        return a * 8 + b * 2 + c if h == 0 else b * 8 + a * 2 + c

    def table_copy(k):
        return pltpu.make_async_remote_copy(
            src_ref=lengths_ref, dst_ref=table_ref.at[dev], send_sem=table_send.at[k],
            recv_sem=table_recv.at[k], device_id=(grp, (dev + k) % slots), device_id_type=MESH)

    ways = (1, 3)
    halves = (0, 1)

    def core_for(j):
        return (core + j) % 2

    far_first = {}
    near_first = {}
    far_second = {}
    for j, way in enumerate(ways):
        for h in halves:
            far_first[h, j] = remote(
                block(h, (at[h][0] + 2) % 4, core_for(j)), turn_first.at[h, j], place(h, way, 0, 0))
    for j, way in enumerate(ways):
        for h in halves:
            near_first[h, j] = remote(
                block(h, (at[h][0] + way) % 4), mid.at[h, 3 - way], place(h, way, 0, 0))
    for j, way in enumerate(ways):
        for h in halves:
            far_second[h, j] = remote(
                turn_first.at[h, j], mid.at[h, 1, :, core_for(j)], place(h, way, 0, 0))

    def last(h, da):
        a, b = at[h]
        origin = (a + da) % 4

        def held(db, c):
            if da == 0:
                return cell(packed_ref, h, a, (b + db) % 4, c)
            return mid.at[h, da - 1, (b + db) % 4, c]

        far = []
        near = []
        for j, way in enumerate(ways):
            first = remote(held(2, core_for(j)), turn_last.at[h, j, da], place(h, 0, way, 0))
            second = remote(
                turn_last.at[h, j, da], cell(recv_ref, h, origin, (b - way) % 4, core),
                place(h, 0, way, j))
            far.append((first, second))
        for way in ways:
            for dc in range(2):
                near.append(remote(
                    held(way, core_for(dc)), cell(recv_ref, h, origin, b, core),
                    place(h, 0, way, dc)))
        near.append(remote(
            held(0, core_for(1)), cell(recv_ref, h, origin, b, core), place(h, 0, 0, 1)))
        own = pltpu.make_async_copy(
            held(0, core), cell(recv_ref, h, origin, b, core), own_sem.at[h, da])
        return far, near, own

    second_stage = {(h, da): last(h, da) for da in range(4) for h in halves}
    own_table = pltpu.make_async_copy(lengths_ref, table_ref.at[dev], own_sem.at[2, 0])
    own_table.start()
    pl.semaphore_wait(barrier, slots - 1)

    for copy in far_first.values():
        copy.start()
    for copy in near_first.values():
        copy.start()

    def send_table(k, carry):
        table_copy(k).start()
        return carry

    lax.fori_loop(1, slots, send_table, 0)

    def begin(h, da):
        far, near, own = second_stage[h, da]
        for first, _ in far:
            first.start()
        for copy in near:
            copy.start()
        own.start()

    def forward(h, da):
        for first, second in second_stage[h, da][0]:
            first.wait_recv()
            second.start()

    for key, copy in far_first.items():
        copy.wait_recv()
        far_second[key].start()
    for h in halves:
        begin(h, 0)
    for j, way in enumerate(ways):
        for h in halves:
            near_first[h, j].wait_recv()
            begin(h, 4 - way)
    for h in halves:
        forward(h, 0)
    for h in halves:
        for j in range(2):
            far_second[h, j].wait_recv()
        begin(h, 2)
    for da in (3, 1, 2):
        for h in halves:
            forward(h, da)
    for h in halves:
        for da in range(4):
            far, near, own = second_stage[h, da]
            for _, second in far:
                second.wait_recv()
            for copy in near:
                copy.wait_recv()
            own.wait()
    for copy in used:
        copy.wait_send()
    own_table.wait()

    def finish(k, carry):
        table_copy(k).wait()
        return carry

    lax.fori_loop(1, slots, finish, 0)


def exchange(counts, packed):
    slots, slot, width = packed.shape
    half = slot // 2
    kind = packed.dtype
    lengths = jnp.broadcast_to(jnp.pad(counts, (0, 128 - slots)), (8, 128))
    shape = (4, 4, 2, 2, half, width)
    copies = 12 + 8 * 9
    received, table = pl.pallas_call(
        exchange_kernel,
        out_shape=(
            jax.ShapeDtypeStruct(shape, kind),
            jax.ShapeDtypeStruct((slots, 8, 128), jnp.int32),
        ),
        in_specs=[
            pl.BlockSpec(memory_space=pltpu.VMEM),
            pl.BlockSpec(memory_space=pl.ANY),
        ],
        out_specs=(pl.BlockSpec(memory_space=pl.ANY), pl.BlockSpec(memory_space=pl.ANY)),
        scratch_shapes=[
            pltpu.VMEM((2, 3, 4, 2, half, width), kind),
            pltpu.VMEM((2, 2, 4, half, width), kind),
            pltpu.VMEM((2, 2, 4, half, width), kind),
            pltpu.SemaphoreType.DMA((slots,)),
            pltpu.SemaphoreType.DMA((slots,)),
            pltpu.SemaphoreType.DMA((copies,)),
            pltpu.SemaphoreType.DMA((copies,)),
            pltpu.SemaphoreType.DMA((3, 4)),
        ],
        compiler_params=pltpu.CompilerParams(collective_id=1, has_side_effects=True),
        name="ring_exchange",
    )(lengths, packed.reshape(shape))
    return received.reshape(slots, slot, width), table


def unpack_kernel(per_step, counts_ref, recv_ref, sensor_ref, power_ref, rows_ref):
    step = pl.program_id(0)
    slot = recv_ref.shape[1]
    owned = power_ref.shape[0]

    def skip(s, total):
        return total + counts_ref[s]

    at = lax.fori_loop(0, step * per_step, skip, jnp.int32(0))
    for i in range(per_step):
        for j in range(2):
            half = recv_ref[i, :, j * NU:(j + 1) * NU]
            rows_ref[j, pl.ds(at, slot), :] = half.astype(jnp.float32)
        at = at + counts_ref[step * per_step + i]

    @pl.when(step == pl.num_programs(0) - 1)
    def _():
        def tile(k, carry):
            here = pl.multiple_of(k * 128, 128)
            power_ref[pl.ds(here, 128), :] = rows_ref[0, pl.ds(here, 128), :].astype(power_ref.dtype)
            block = rows_ref[1, pl.ds(here, 128), :]
            sensor_ref[:, pl.ds(here, 128)] = block.T.astype(sensor_ref.dtype)
            return carry

        lax.fori_loop(0, owned // 128, tile, 0)


def unpack(counts, recv, owned):
    per_step = 4
    slots, slot, width = recv.shape
    return pl.pallas_call(
        functools.partial(unpack_kernel, per_step),
        out_shape=(
            jax.ShapeDtypeStruct((NU, owned), recv.dtype),
            jax.ShapeDtypeStruct((owned, NU), recv.dtype),
        ),
        grid_spec=pltpu.PrefetchScalarGridSpec(
            num_scalar_prefetch=1,
            grid=(slots // per_step,),
            in_specs=[pl.BlockSpec((per_step, slot, width), lambda i, c: (i, 0, 0))],
            out_specs=(
                pl.BlockSpec((NU, owned), lambda i, c: (0, 0)),
                pl.BlockSpec((owned, NU), lambda i, c: (0, 0)),
            ),
            scratch_shapes=[pltpu.VMEM((2, owned + slot, NU), jnp.float32)],
        ),
        name="unpack_rows",
    )(counts, recv)


def corr_kernel(scale, sensor_ref, power_ref, out_ref, *scratch):
    (wide, landed, rows, shifted, head, ex_send, ex_recv, edge_send, edge_recv,
     rs_send, rs_recv) = scratch[:11]
    acc = scratch[11:17]
    got = scratch[17:23]
    owned = power_ref.shape[0]
    total = 2 * owned
    grp = lax.axis_index("grp")
    dev = lax.axis_index("dev")
    core = dev % 2
    chip = dev // 2
    y = chip % 4
    x = chip // 4
    partner = (grp, dev + 1 - 2 * core)
    after = (chip + 1) % 16
    before = (chip + 15) % 16

    def place(xx, yy, zz):
        return (zz, xx * 8 + yy * 2 + core)

    def near(a):
        return a + 1 - 2 * (a % 2)

    def far(a):
        return 3 - a

    neighbours = (
        place(near(x), y, grp), place(x, near(y), grp), place(x, y, near(grp)),
        place(far(x), y, grp), place(x, far(y), grp), place(x, y, far(grp)),
    )

    def near_bit(a):
        return (a // 2 + a % 2) % 2

    own_bits = (near_bit(x), near_bit(y), near_bit(grp), x // 2, y // 2, grp // 2)

    barrier = pltpu.get_barrier_semaphore()

    def greet(target):
        pl.semaphore_signal(barrier, inc=1, device_id=target, device_id_type=MESH)

    greet(partner)
    for target in neighbours:
        greet(target)
    greet((grp, before * 2 + 1))
    greet((grp, after * 2))
    greet((grp, jnp.where(core == 1, after * 2 + 1, before * 2)))
    pl.semaphore_wait(barrier, 10)

    own_at = pl.multiple_of(core * owned, 128)
    here = (
        (sensor_ref, wide.at[0:NU, pl.ds(own_at, owned)]),
        (power_ref, landed.at[pl.ds(pl.multiple_of(HALO + core * owned, 128), owned), :]),
    )
    exchange = [
        pltpu.make_async_remote_copy(
            src_ref=src, dst_ref=dst, send_sem=ex_send.at[i], recv_sem=ex_recv.at[i],
            device_id=partner, device_id_type=MESH)
        for i, (src, dst) in enumerate(here)
    ]
    edges = (
        (sensor_ref.at[:, 0:128], head, before),
        (power_ref.at[pl.ds(owned - HALO, HALO), :], landed.at[0:HALO, :], after),
    )

    def edge_copy(i, which):
        src, dst, target = edges[i]
        return pltpu.make_async_remote_copy(
            src_ref=src, dst_ref=dst, send_sem=edge_send.at[which], recv_sem=edge_recv.at[i],
            device_id=(grp, target * 2 + which), device_id_type=MESH)

    for i in range(2):
        @pl.when(core == i)
        def _(i=i):
            for which in range(2):
                edge_copy(i, which).start()

    for copy in exchange:
        copy.start()
    wide[0:NU, pl.ds(own_at, owned)] = sensor_ref[...]
    power_at = pl.multiple_of(HALO + core * owned, 128)
    rows[pl.ds(power_at, owned), :] = power_ref[...].astype(jnp.float32)
    exchange[1].wait_recv()
    other_at = pl.multiple_of(HALO + (1 - core) * owned, 128)
    rows[pl.ds(other_at, owned), :] = landed[pl.ds(other_at, owned), :].astype(jnp.float32)
    edge_copy(1, 0).wait_recv()
    rows[0:HALO, :] = jnp.where(chip > 0, landed[0:HALO, :].astype(jnp.float32), 0.0)

    def shift_rows(k, carry):
        at = pl.multiple_of(k * 912, 16)
        for u in range(4):
            shifted[u, pl.ds(at, 912), :] = rows[
                pl.ds(at + 16 - 4 * u - 2 * core, 912), :].astype(shifted.dtype)
        return carry

    lax.fori_loop(0, (LEAD + total) // 912, shift_rows, 0)

    edge_copy(0, 0).wait_recv()
    exchange[0].wait_recv()
    lane = lax.broadcasted_iota(jnp.int32, (NU, 128), 1)

    def turn(block):
        return pltpu.roll(block.astype(jnp.float32), 127, 1)

    def shift_lanes(k, following):
        at = pl.multiple_of(total - 128 - k * 128, 128)
        turned = turn(wide[0:NU, pl.ds(at, 128)])
        wide[NU:2 * NU, pl.ds(at, 128)] = jnp.where(lane == 127, following, turned).astype(wide.dtype)
        return turned

    lax.fori_loop(0, total // 128, shift_lanes, jnp.where(chip < 15, turn(head[...]), 0.0))

    def step_copy(step, q, src, dst):
        return pltpu.make_async_remote_copy(
            src_ref=src, dst_ref=dst, send_sem=rs_send.at[step, q], recv_sem=rs_recv.at[step, q],
            device_id=neighbours[(q + step) % DIMS], device_id_type=MESH)

    def read_at(bits):
        flip = [(o + b) % 2 for o, b in zip(own_bits, bits)]
        xd, yd, zd = (2 * flip[3 + i] + (flip[i] + flip[3 + i]) % 2 for i in range(3))
        return yd, pl.multiple_of(LEAD - 16 * (zd * 4 + xd), 16)

    def pair(i, carry):
        first = BLOCKS - 1 - 2 * i
        both = []
        for block in (first, first - 1):
            bits = [(block // 2 ** b) % 2 for b in range(DIMS)]
            both.append((bits, read_at(bits)))
        result = None
        for k in range(0, total, K_CHUNK):
            operand = jnp.concatenate(
                [shifted[u, pl.ds(at + k, K_CHUNK), :] for _, (u, at) in both], axis=1)
            term = jnp.dot(wide[:, k:k + K_CHUNK], operand, preferred_element_type=jnp.float32)
            result = term if result is None else result + term
        for j, (bits, _) in enumerate(both):
            for q in range(DIMS):
                index = sum(bits[(q + e) % DIMS] * 2 ** (DIMS - 1 - e) for e in range(DIMS))
                acc[q][index] = result[PART_AT[q]:PART_AT[q] + PARTS[q], j * NU:(j + 1) * NU]

                @pl.when(bits[q] == 1)
                def _(q=q, index=index):
                    step_copy(0, q, acc[q].at[index], got[q].at[index - BLOCKS // 2]).start()
        return carry

    lax.fori_loop(0, BLOCKS // 2, pair, 0)

    sent = [[step_copy(0, q, acc[q].at[32:64], got[q].at[0:32]) for q in range(DIMS)]]
    begin = 0
    for step in range(1, DIMS):
        n = 2 ** (DIMS - 1 - step)
        copies = []
        for q in range(DIMS):
            sent[step - 1][q].wait_recv()
            acc[q][n:2 * n] = acc[q][n:2 * n] + got[q][begin + n:begin + 2 * n]
            copy = step_copy(
                step, q, acc[q].at[n:2 * n], got[q].at[begin + 2 * n:begin + 3 * n])
            copy.start()
            copies.append(copy)
        for q in range(DIMS):
            acc[q][0:n] = acc[q][0:n] + got[q][begin:begin + n]
        sent.append(copies)
        begin += 2 * n
    for q in range(DIMS):
        sent[DIMS - 1][q].wait_recv()
        out_ref[PART_AT[q]:PART_AT[q] + PARTS[q], :] = (acc[q][0] + got[q][begin]) * scale

    for copies in sent:
        for copy in copies:
            copy.wait_send()
    for copy in exchange:
        copy.wait_send()

    for i in range(2):
        @pl.when(core == i)
        def _(i=i):
            for which in range(2):
                edge_copy(i, which).wait_send()


def correlate(sensor, power, scale):
    owned = power.shape[0]
    total = 2 * owned
    kind = power.dtype
    return pl.pallas_call(
        functools.partial(corr_kernel, scale),
        out_shape=jax.ShapeDtypeStruct((2 * NU, NU), jnp.float32),
        in_specs=[pl.BlockSpec(memory_space=pltpu.VMEM)] * 2,
        out_specs=pl.BlockSpec(memory_space=pltpu.VMEM),
        scratch_shapes=[
            pltpu.VMEM((2 * NU, total), kind),
            pltpu.VMEM((HALO + total, NU), kind),
            pltpu.VMEM((HALO + total, NU), jnp.float32),
            pltpu.VMEM((4, LEAD + total, NU), kind),
            pltpu.VMEM((NU, 128), kind),
            pltpu.SemaphoreType.DMA((2,)),
            pltpu.SemaphoreType.DMA((2,)),
            pltpu.SemaphoreType.DMA((2,)),
            pltpu.SemaphoreType.DMA((2,)),
            pltpu.SemaphoreType.DMA((DIMS, DIMS)),
            pltpu.SemaphoreType.DMA((DIMS, DIMS)),
        ]
        + [pltpu.VMEM((BLOCKS, h, NU), jnp.float32) for h in PARTS]
        + [pltpu.VMEM((BLOCKS - 1, h, NU), jnp.float32) for h in PARTS],
        compiler_params=pltpu.CompilerParams(
            collective_id=0, has_side_effects=True, vmem_limit_bytes=56 << 20),
        name="correlate_scatter",
    )(sensor, power)


def per_device(trace, counts):
    dev_count = lax.axis_size("dev")
    group_count = lax.axis_size("grp")
    capacity = trace.shape[0]
    slot_rows = capacity // dev_count
    owned = capacity // 2
    send_counts = counts.reshape(-1)
    received, table = exchange(send_counts, pack(send_counts, trace, dev_count, slot_rows))
    recv_counts = lax.dynamic_index_in_dim(table[:, 0, :], lax.axis_index("dev"), 1, False)
    sensor, power = unpack(recv_counts, received, owned)
    scale = 1.0 / math.sqrt(group_count * dev_count * owned)
    return correlate(sensor, power, scale).reshape(2, NU, NU)


def solution(mesh):
    in_specs = (P(("grp", "dev"), None), P("grp", "dev", None))
    out_specs = P(("grp", "dev"), None, None)
    return jax.shard_map(
        per_device, mesh=mesh, in_specs=in_specs, out_specs=out_specs, check_vma=False
    )
```

```python
import functools
import math

import jax
import jax.numpy as jnp
from jax import lax
from jax.experimental import pallas as pl
from jax.experimental.pallas import tpu as pltpu
from jax.sharding import PartitionSpec as P

NU = 128
LAGS = 256
MESH = pl.DeviceIdType.MESH
DIMS = 6
BLOCKS = 64
HALO = 256
LEAD = 240
PARTS = (48, 40, 40, 48, 40, 40)
PART_AT = (0, 48, 88, 128, 176, 216)
K_CHUNK = 2048
BEHIND = 5


def pack_kernel(per_step, slot, counts_ref, trace_ref, out_ref, rows_ref):
    step = pl.program_id(0)
    capacity = trace_ref.shape[0]
    top = capacity - slot - 16

    def skip(d, total):
        return total + counts_ref[d]

    start = lax.fori_loop(0, step * per_step, skip, jnp.int32(0))
    for i in range(per_step):
        base = pl.multiple_of(jnp.minimum(start // 16 * 16, top), 16)
        for j in range(2):
            half = slice(j * NU, (j + 1) * NU)
            rows_ref[i, j] = trace_ref[pl.ds(base, slot + 16), half].astype(jnp.float32)
            out_ref[i, :, half] = rows_ref[i, j, pl.ds(start - base, slot), :].astype(out_ref.dtype)
        start = start + counts_ref[step * per_step + i]


def pack(counts, trace, slots, slot):
    per_step = 4
    return pl.pallas_call(
        functools.partial(pack_kernel, per_step, slot),
        out_shape=jax.ShapeDtypeStruct((slots, slot, trace.shape[1]), trace.dtype),
        grid_spec=pltpu.PrefetchScalarGridSpec(
            num_scalar_prefetch=1,
            grid=(slots // per_step,),
            in_specs=[pl.BlockSpec(trace.shape, lambda i, c: (0, 0))],
            out_specs=pl.BlockSpec((per_step, slot, trace.shape[1]), lambda i, c: (i, 0, 0)),
            scratch_shapes=[pltpu.VMEM((per_step, 2, slot + 16, NU), jnp.float32)],
        ),
        name="pack_rows",
    )(counts, trace)


def exchange_kernel(lengths_ref, packed_ref, recv_ref, table_ref, mid, turn_first, turn_last,
                    table_send, table_recv, send_sem, recv_sem, own_sem):
    slots = table_ref.shape[0]
    grp = lax.axis_index("grp")
    dev = lax.axis_index("dev")
    core = dev % 2
    y = dev // 2 % 4
    x = dev // 8
    barrier = pltpu.get_barrier_semaphore()

    def greet(k, carry):
        pl.semaphore_signal(barrier, inc=1, device_id=(grp, (dev + k) % slots), device_id_type=MESH)
        return carry

    lax.fori_loop(1, slots, greet, 0)
    used = []

    def remote(src, dst, target):
        i = len(used)
        copy = pltpu.make_async_remote_copy(
            src_ref=src, dst_ref=dst, send_sem=send_sem.at[i], recv_sem=recv_sem.at[i],
            device_id=(grp, target), device_id_type=MESH)
        used.append(copy)
        return copy

    def cell(ref, h, a, b, c):
        return ref.at[a, b, c, h] if h == 0 else ref.at[b, a, c, h]

    def block(h, a, c=slice(None)):
        return packed_ref.at[a, :, c, h] if h == 0 else packed_ref.at[:, a, c, h]

    at = ((x, y), (y, x))

    def place(h, da, db, dc):
        a = (at[h][0] + da) % 4
        b = (at[h][1] + db) % 4
        c = (core + dc) % 2
        return a * 8 + b * 2 + c if h == 0 else b * 8 + a * 2 + c

    def table_copy(k):
        return pltpu.make_async_remote_copy(
            src_ref=lengths_ref, dst_ref=table_ref.at[dev], send_sem=table_send.at[k],
            recv_sem=table_recv.at[k], device_id=(grp, (dev + k) % slots), device_id_type=MESH)

    ways = (1, 3)
    halves = (0, 1)

    def core_for(j):
        return (core + j) % 2

    far_first = {}
    near_first = {}
    far_second = {}
    for j, way in enumerate(ways):
        for h in halves:
            far_first[h, j] = remote(
                block(h, (at[h][0] + 2) % 4, core_for(j)), turn_first.at[h, j], place(h, way, 0, 0))
    for j, way in enumerate(ways):
        for h in halves:
            near_first[h, j] = remote(
                block(h, (at[h][0] + way) % 4), mid.at[h, 3 - way], place(h, way, 0, 0))
    for j, way in enumerate(ways):
        for h in halves:
            far_second[h, j] = remote(
                turn_first.at[h, j], mid.at[h, 1, :, core_for(j)], place(h, way, 0, 0))

    def last(h, da):
        a, b = at[h]
        origin = (a + da) % 4

        def held(db, c):
            if da == 0:
                return cell(packed_ref, h, a, (b + db) % 4, c)
            return mid.at[h, da - 1, (b + db) % 4, c]

        far = []
        near = []
        for j, way in enumerate(ways):
            first = remote(held(2, core_for(j)), turn_last.at[h, j, da], place(h, 0, way, 0))
            second = remote(
                turn_last.at[h, j, da], cell(recv_ref, h, origin, (b - way) % 4, core),
                place(h, 0, way, j))
            far.append((first, second))
        for way in ways:
            for dc in range(2):
                near.append(remote(
                    held(way, core_for(dc)), cell(recv_ref, h, origin, b, core),
                    place(h, 0, way, dc)))
        near.append(remote(
            held(0, core_for(1)), cell(recv_ref, h, origin, b, core), place(h, 0, 0, 1)))
        own = pltpu.make_async_copy(
            held(0, core), cell(recv_ref, h, origin, b, core), own_sem.at[h, da])
        return far, near, own

    second_stage = {(h, da): last(h, da) for da in range(4) for h in halves}
    own_table = pltpu.make_async_copy(lengths_ref, table_ref.at[dev], own_sem.at[2, 0])
    own_table.start()
    pl.semaphore_wait(barrier, slots - 1)

    for copy in far_first.values():
        copy.start()
    for copy in near_first.values():
        copy.start()

    def send_table(k, carry):
        table_copy(k).start()
        return carry

    lax.fori_loop(1, slots, send_table, 0)

    def begin(h, da):
        far, near, own = second_stage[h, da]
        for first, _ in far:
            first.start()
        for copy in near:
            copy.start()
        own.start()

    def forward(h, da):
        for first, second in second_stage[h, da][0]:
            first.wait_recv()
            second.start()

    for key, copy in far_first.items():
        copy.wait_recv()
        far_second[key].start()
    for h in halves:
        begin(h, 0)
    for j, way in enumerate(ways):
        for h in halves:
            near_first[h, j].wait_recv()
            begin(h, 4 - way)
    for h in halves:
        forward(h, 0)
    for h in halves:
        for j in range(2):
            far_second[h, j].wait_recv()
        begin(h, 2)
    for da in (3, 1, 2):
        for h in halves:
            forward(h, da)
    for h in halves:
        for da in range(4):
            far, near, own = second_stage[h, da]
            for _, second in far:
                second.wait_recv()
            for copy in near:
                copy.wait_recv()
            own.wait()
    for copy in used:
        copy.wait_send()
    own_table.wait()

    def finish(k, carry):
        table_copy(k).wait()
        return carry

    lax.fori_loop(1, slots, finish, 0)


def exchange(counts, packed):
    slots, slot, width = packed.shape
    half = slot // 2
    kind = packed.dtype
    lengths = jnp.broadcast_to(jnp.pad(counts, (0, 128 - slots)), (8, 128))
    shape = (4, 4, 2, 2, half, width)
    copies = 12 + 8 * 9
    received, table = pl.pallas_call(
        exchange_kernel,
        out_shape=(
            jax.ShapeDtypeStruct(shape, kind),
            jax.ShapeDtypeStruct((slots, 8, 128), jnp.int32),
        ),
        in_specs=[
            pl.BlockSpec(memory_space=pltpu.VMEM),
            pl.BlockSpec(memory_space=pl.ANY),
        ],
        out_specs=(pl.BlockSpec(memory_space=pl.ANY), pl.BlockSpec(memory_space=pl.ANY)),
        scratch_shapes=[
            pltpu.VMEM((2, 3, 4, 2, half, width), kind),
            pltpu.VMEM((2, 2, 4, half, width), kind),
            pltpu.VMEM((2, 2, 4, half, width), kind),
            pltpu.SemaphoreType.DMA((slots,)),
            pltpu.SemaphoreType.DMA((slots,)),
            pltpu.SemaphoreType.DMA((copies,)),
            pltpu.SemaphoreType.DMA((copies,)),
            pltpu.SemaphoreType.DMA((3, 4)),
        ],
        compiler_params=pltpu.CompilerParams(collective_id=1, has_side_effects=True),
        name="ring_exchange",
    )(lengths, packed.reshape(shape))
    return received.reshape(slots, slot, width), table


def unpack_kernel(per_step, counts_ref, recv_ref, sensor_ref, power_ref, rows_ref):
    step = pl.program_id(0)
    slot = recv_ref.shape[1]
    owned = power_ref.shape[0]

    def skip(s, total):
        return total + counts_ref[s]

    at = lax.fori_loop(0, step * per_step, skip, jnp.int32(0))
    for i in range(per_step):
        for j in range(2):
            half = recv_ref[i, :, j * NU:(j + 1) * NU]
            rows_ref[j, pl.ds(at, slot), :] = half.astype(jnp.float32)
        at = at + counts_ref[step * per_step + i]

    @pl.when(step == pl.num_programs(0) - 1)
    def _():
        def tile(k, carry):
            here = pl.multiple_of(k * 128, 128)
            power_ref[pl.ds(here, 128), :] = rows_ref[0, pl.ds(here, 128), :].astype(power_ref.dtype)
            block = rows_ref[1, pl.ds(here, 128), :]
            sensor_ref[:, pl.ds(here, 128)] = block.T.astype(sensor_ref.dtype)
            return carry

        lax.fori_loop(0, owned // 128, tile, 0)


def unpack(counts, recv, owned):
    per_step = 4
    slots, slot, width = recv.shape
    return pl.pallas_call(
        functools.partial(unpack_kernel, per_step),
        out_shape=(
            jax.ShapeDtypeStruct((NU, owned), recv.dtype),
            jax.ShapeDtypeStruct((owned, NU), recv.dtype),
        ),
        grid_spec=pltpu.PrefetchScalarGridSpec(
            num_scalar_prefetch=1,
            grid=(slots // per_step,),
            in_specs=[pl.BlockSpec((per_step, slot, width), lambda i, c: (i, 0, 0))],
            out_specs=(
                pl.BlockSpec((NU, owned), lambda i, c: (0, 0)),
                pl.BlockSpec((owned, NU), lambda i, c: (0, 0)),
            ),
            scratch_shapes=[pltpu.VMEM((2, owned + slot, NU), jnp.float32)],
        ),
        name="unpack_rows",
    )(counts, recv)


def corr_kernel(scale, sensor_ref, power_ref, out_ref, *scratch):
    (wide, landed, rows, shifted, head, ex_send, ex_recv, edge_send, edge_recv,
     rs_send, rs_recv, first_recv) = scratch[:12]
    acc = scratch[12:18]
    got = scratch[18:24]
    owned = power_ref.shape[0]
    total = 2 * owned
    grp = lax.axis_index("grp")
    dev = lax.axis_index("dev")
    core = dev % 2
    chip = dev // 2
    y = chip % 4
    x = chip // 4
    partner = (grp, dev + 1 - 2 * core)
    after = (chip + 1) % 16
    before = (chip + 15) % 16

    def place(xx, yy, zz):
        return (zz, xx * 8 + yy * 2 + core)

    def near(a):
        return a + 1 - 2 * (a % 2)

    def far(a):
        return 3 - a

    neighbours = (
        place(near(x), y, grp), place(x, near(y), grp), place(x, y, near(grp)),
        place(far(x), y, grp), place(x, far(y), grp), place(x, y, far(grp)),
    )

    def near_bit(a):
        return (a // 2 + a % 2) % 2

    own_bits = (near_bit(x), near_bit(y), near_bit(grp), x // 2, y // 2, grp // 2)

    barrier = pltpu.get_barrier_semaphore()

    def greet(target):
        pl.semaphore_signal(barrier, inc=1, device_id=target, device_id_type=MESH)

    greet(partner)
    for target in neighbours:
        greet(target)
    greet((grp, before * 2 + 1))
    greet((grp, after * 2))
    greet((grp, jnp.where(core == 1, after * 2 + 1, before * 2)))
    pl.semaphore_wait(barrier, 10)

    own_at = pl.multiple_of(core * owned, 128)
    here = (
        (sensor_ref, wide.at[0:NU, pl.ds(own_at, owned)]),
        (power_ref, landed.at[pl.ds(pl.multiple_of(HALO + core * owned, 128), owned), :]),
    )
    exchange = [
        pltpu.make_async_remote_copy(
            src_ref=src, dst_ref=dst, send_sem=ex_send.at[i], recv_sem=ex_recv.at[i],
            device_id=partner, device_id_type=MESH)
        for i, (src, dst) in enumerate(here)
    ]
    edges = (
        (sensor_ref.at[:, 0:128], head, before),
        (power_ref.at[pl.ds(owned - HALO, HALO), :], landed.at[0:HALO, :], after),
    )

    def edge_copy(i, which):
        src, dst, target = edges[i]
        return pltpu.make_async_remote_copy(
            src_ref=src, dst_ref=dst, send_sem=edge_send.at[which], recv_sem=edge_recv.at[i],
            device_id=(grp, target * 2 + which), device_id_type=MESH)

    for i in range(2):
        @pl.when(core == i)
        def _(i=i):
            for which in range(2):
                edge_copy(i, which).start()

    for copy in exchange:
        copy.start()
    wide[0:NU, pl.ds(own_at, owned)] = sensor_ref[...]
    power_at = pl.multiple_of(HALO + core * owned, 128)
    rows[pl.ds(power_at, owned), :] = power_ref[...].astype(jnp.float32)
    exchange[1].wait_recv()
    other_at = pl.multiple_of(HALO + (1 - core) * owned, 128)
    rows[pl.ds(other_at, owned), :] = landed[pl.ds(other_at, owned), :].astype(jnp.float32)
    edge_copy(1, 0).wait_recv()
    rows[0:HALO, :] = jnp.where(chip > 0, landed[0:HALO, :].astype(jnp.float32), 0.0)

    def shift_rows(k, carry):
        at = pl.multiple_of(k * 912, 16)
        for u in range(4):
            shifted[u, pl.ds(at, 912), :] = rows[
                pl.ds(at + 16 - 4 * u - 2 * core, 912), :].astype(shifted.dtype)
        return carry

    lax.fori_loop(0, (LEAD + total) // 912, shift_rows, 0)

    edge_copy(0, 0).wait_recv()
    exchange[0].wait_recv()
    lane = lax.broadcasted_iota(jnp.int32, (NU, 128), 1)

    def turn(block):
        return pltpu.roll(block.astype(jnp.float32), 127, 1)

    def shift_lanes(k, following):
        at = pl.multiple_of(total - 128 - k * 128, 128)
        turned = turn(wide[0:NU, pl.ds(at, 128)])
        wide[NU:2 * NU, pl.ds(at, 128)] = jnp.where(lane == 127, following, turned).astype(wide.dtype)
        return turned

    lax.fori_loop(0, total // 128, shift_lanes, jnp.where(chip < 15, turn(head[...]), 0.0))

    def step_copy(step, q, src, dst):
        return pltpu.make_async_remote_copy(
            src_ref=src, dst_ref=dst, send_sem=rs_send.at[step, q], recv_sem=rs_recv.at[step, q],
            device_id=neighbours[(q + step) % DIMS], device_id_type=MESH)

    def read_at(bits):
        flip = [(o + b) % 2 for o, b in zip(own_bits, bits)]
        xd, yd, zd = (2 * flip[3 + i] + (flip[i] + flip[3 + i]) % 2 for i in range(3))
        return yd, pl.multiple_of(LEAD - 16 * (zd * 4 + xd), 16)

    def first_copy(q, index):
        slot = index % (BLOCKS // 2)
        return pltpu.make_async_remote_copy(
            src_ref=acc[q].at[slot + BLOCKS // 2], dst_ref=got[q].at[slot],
            send_sem=rs_send.at[0, q], recv_sem=first_recv.at[q, slot],
            device_id=neighbours[q], device_id_type=MESH)

    def bits_of(i):
        first = BLOCKS - 1 - 2 * i
        return [
            [1 - j] + [(first // 2 ** b) % 2 for b in range(1, DIMS)] for j in range(2)]

    def index_of(q, bits):
        return sum(bits[(q + e) % DIMS] * 2 ** (DIMS - 1 - e) for e in range(DIMS))

    def follow(i):
        both = bits_of(i)

        def take(q, j):
            index = index_of(q, both[j]) % (BLOCKS // 2)
            first_copy(q, index).wait_recv()
            acc[q][index] = acc[q][index] + got[q][index]
            return index

        def pass_on(q, index):
            low = index % (BLOCKS // 4)
            step_copy(
                1, q, acc[q].at[low + BLOCKS // 4], got[q].at[low + BLOCKS // 2]).start()

        for q in range(DIMS):
            which = (1,) if q == 0 else (0, 1)

            def step(q=q, which=which):
                taken = [take(q, j) for j in which]
                if q == DIMS - 1:
                    pass_on(q, taken[0])
                else:
                    @pl.when(both[0][q + 1] == 1)
                    def _():
                        for index in taken:
                            pass_on(q, index)

            if q == 0:
                step()
            else:
                pl.when(both[0][q] == 0)(step)

    def pair(i, carry):
        both = bits_of(i)
        reads = [read_at(bits) for bits in both]
        result = None
        for k in range(0, total, K_CHUNK):
            operand = jnp.concatenate(
                [shifted[u, pl.ds(at + k, K_CHUNK), :] for u, at in reads], axis=1)
            term = jnp.dot(wide[:, k:k + K_CHUNK], operand, preferred_element_type=jnp.float32)
            result = term if result is None else result + term
        for q in range(DIMS):
            for j in range(2):
                acc[q][index_of(q, both[j])] = result[
                    PART_AT[q]:PART_AT[q] + PARTS[q], j * NU:(j + 1) * NU]
            if q == 0:
                first_copy(q, index_of(q, both[0])).start()
            else:
                @pl.when(both[0][q] == 1)
                def _(q=q):
                    for j in range(2):
                        first_copy(q, index_of(q, both[j])).start()

        @pl.when(i >= BEHIND)
        def _():
            follow(i - BEHIND)

        return carry

    lax.fori_loop(0, BLOCKS // 2, pair, 0)

    def rest(i, carry):
        follow(i)
        return carry

    lax.fori_loop(BLOCKS // 2 - BEHIND, BLOCKS // 2, rest, 0)

    sent = [
        [step_copy(0, q, acc[q].at[32:64], got[q].at[0:32]) for q in range(DIMS)],
        [step_copy(1, q, acc[q].at[16:32], got[q].at[32:48]) for q in range(DIMS)],
    ]
    begin = BLOCKS // 2
    for step in range(2, DIMS):
        n = 2 ** (DIMS - 1 - step)
        copies = []
        for q in range(DIMS):
            sent[step - 1][q].wait_recv()
            acc[q][n:2 * n] = acc[q][n:2 * n] + got[q][begin + n:begin + 2 * n]
            copy = step_copy(
                step, q, acc[q].at[n:2 * n], got[q].at[begin + 2 * n:begin + 3 * n])
            copy.start()
            copies.append(copy)
        for q in range(DIMS):
            acc[q][0:n] = acc[q][0:n] + got[q][begin:begin + n]
        sent.append(copies)
        begin += 2 * n
    for q in range(DIMS):
        sent[DIMS - 1][q].wait_recv()
        out_ref[PART_AT[q]:PART_AT[q] + PARTS[q], :] = (acc[q][0] + got[q][begin]) * scale

    for copies in sent:
        for copy in copies:
            copy.wait_send()
    for copy in exchange:
        copy.wait_send()

    for i in range(2):
        @pl.when(core == i)
        def _(i=i):
            for which in range(2):
                edge_copy(i, which).wait_send()


def correlate(sensor, power, scale):
    owned = power.shape[0]
    total = 2 * owned
    kind = power.dtype
    return pl.pallas_call(
        functools.partial(corr_kernel, scale),
        out_shape=jax.ShapeDtypeStruct((2 * NU, NU), jnp.float32),
        in_specs=[pl.BlockSpec(memory_space=pltpu.VMEM)] * 2,
        out_specs=pl.BlockSpec(memory_space=pltpu.VMEM),
        scratch_shapes=[
            pltpu.VMEM((2 * NU, total), kind),
            pltpu.VMEM((HALO + total, NU), kind),
            pltpu.VMEM((HALO + total, NU), jnp.float32),
            pltpu.VMEM((4, LEAD + total, NU), kind),
            pltpu.VMEM((NU, 128), kind),
            pltpu.SemaphoreType.DMA((2,)),
            pltpu.SemaphoreType.DMA((2,)),
            pltpu.SemaphoreType.DMA((2,)),
            pltpu.SemaphoreType.DMA((2,)),
            pltpu.SemaphoreType.DMA((DIMS, DIMS)),
            pltpu.SemaphoreType.DMA((DIMS, DIMS)),
            pltpu.SemaphoreType.DMA((DIMS, BLOCKS // 2)),
        ]
        + [pltpu.VMEM((BLOCKS, h, NU), jnp.float32) for h in PARTS]
        + [pltpu.VMEM((BLOCKS - 1, h, NU), jnp.float32) for h in PARTS],
        compiler_params=pltpu.CompilerParams(
            collective_id=0, has_side_effects=True, vmem_limit_bytes=56 << 20),
        name="correlate_scatter",
    )(sensor, power)


def per_device(trace, counts):
    dev_count = lax.axis_size("dev")
    group_count = lax.axis_size("grp")
    capacity = trace.shape[0]
    slot_rows = capacity // dev_count
    owned = capacity // 2
    send_counts = counts.reshape(-1)
    received, table = exchange(send_counts, pack(send_counts, trace, dev_count, slot_rows))
    recv_counts = lax.dynamic_index_in_dim(table[:, 0, :], lax.axis_index("dev"), 1, False)
    sensor, power = unpack(recv_counts, received, owned)
    scale = 1.0 / math.sqrt(group_count * dev_count * owned)
    return correlate(sensor, power, scale).reshape(2, NU, NU)


def solution(mesh):
    in_specs = (P(("grp", "dev"), None), P("grp", "dev", None))
    out_specs = P(("grp", "dev"), None, None)
    return jax.shard_map(
        per_device, mesh=mesh, in_specs=in_specs, out_specs=out_specs, check_vma=False
    )
```

```python
import functools
import math

import jax
import jax.numpy as jnp
from jax import lax
from jax.experimental import pallas as pl
from jax.experimental.pallas import tpu as pltpu
from jax.sharding import PartitionSpec as P

NU = 128
LAGS = 256
MESH = pl.DeviceIdType.MESH
DIMS = 6
BLOCKS = 64
HALO = 256
LEAD = 240
PARTS = (48, 40, 40, 48, 40, 40)
PART_AT = (0, 48, 88, 128, 176, 216)
K_CHUNK = 2048
BEHIND = 8


def pack_kernel(per_step, slot, counts_ref, trace_ref, out_ref, rows_ref):
    step = pl.program_id(0)
    capacity = trace_ref.shape[0]
    top = capacity - slot - 16

    def skip(d, total):
        return total + counts_ref[d]

    start = lax.fori_loop(0, step * per_step, skip, jnp.int32(0))
    for i in range(per_step):
        base = pl.multiple_of(jnp.minimum(start // 16 * 16, top), 16)
        for j in range(2):
            half = slice(j * NU, (j + 1) * NU)
            rows_ref[i, j] = trace_ref[pl.ds(base, slot + 16), half].astype(jnp.float32)
            out_ref[i, :, half] = rows_ref[i, j, pl.ds(start - base, slot), :].astype(out_ref.dtype)
        start = start + counts_ref[step * per_step + i]


def pack(counts, trace, slots, slot):
    per_step = 4
    return pl.pallas_call(
        functools.partial(pack_kernel, per_step, slot),
        out_shape=jax.ShapeDtypeStruct((slots, slot, trace.shape[1]), trace.dtype),
        grid_spec=pltpu.PrefetchScalarGridSpec(
            num_scalar_prefetch=1,
            grid=(slots // per_step,),
            in_specs=[pl.BlockSpec(trace.shape, lambda i, c: (0, 0))],
            out_specs=pl.BlockSpec((per_step, slot, trace.shape[1]), lambda i, c: (i, 0, 0)),
            scratch_shapes=[pltpu.VMEM((per_step, 2, slot + 16, NU), jnp.float32)],
        ),
        name="pack_rows",
    )(counts, trace)


def exchange_kernel(lengths_ref, packed_ref, recv_ref, table_ref, mid, turn_first, turn_last,
                    table_send, table_recv, send_sem, recv_sem, own_sem):
    slots = table_ref.shape[0]
    grp = lax.axis_index("grp")
    dev = lax.axis_index("dev")
    core = dev % 2
    y = dev // 2 % 4
    x = dev // 8
    barrier = pltpu.get_barrier_semaphore()

    def greet(k, carry):
        pl.semaphore_signal(barrier, inc=1, device_id=(grp, (dev + k) % slots), device_id_type=MESH)
        return carry

    lax.fori_loop(1, slots, greet, 0)
    used = []

    def remote(src, dst, target):
        i = len(used)
        copy = pltpu.make_async_remote_copy(
            src_ref=src, dst_ref=dst, send_sem=send_sem.at[i], recv_sem=recv_sem.at[i],
            device_id=(grp, target), device_id_type=MESH)
        used.append(copy)
        return copy

    def cell(ref, h, a, b, c):
        return ref.at[a, b, c, h] if h == 0 else ref.at[b, a, c, h]

    def block(h, a, c=slice(None)):
        return packed_ref.at[a, :, c, h] if h == 0 else packed_ref.at[:, a, c, h]

    at = ((x, y), (y, x))

    def place(h, da, db, dc):
        a = (at[h][0] + da) % 4
        b = (at[h][1] + db) % 4
        c = (core + dc) % 2
        return a * 8 + b * 2 + c if h == 0 else b * 8 + a * 2 + c

    def table_copy(k):
        return pltpu.make_async_remote_copy(
            src_ref=lengths_ref, dst_ref=table_ref.at[dev], send_sem=table_send.at[k],
            recv_sem=table_recv.at[k], device_id=(grp, (dev + k) % slots), device_id_type=MESH)

    ways = (1, 3)
    halves = (0, 1)

    def core_for(j):
        return (core + j) % 2

    far_first = {}
    near_first = {}
    far_second = {}
    for j, way in enumerate(ways):
        for h in halves:
            far_first[h, j] = remote(
                block(h, (at[h][0] + 2) % 4, core_for(j)), turn_first.at[h, j], place(h, way, 0, 0))
    for j, way in enumerate(ways):
        for h in halves:
            near_first[h, j] = remote(
                block(h, (at[h][0] + way) % 4), mid.at[h, 3 - way], place(h, way, 0, 0))
    for j, way in enumerate(ways):
        for h in halves:
            far_second[h, j] = remote(
                turn_first.at[h, j], mid.at[h, 1, :, core_for(j)], place(h, way, 0, 0))

    def last(h, da):
        a, b = at[h]
        origin = (a + da) % 4

        def held(db, c):
            if da == 0:
                return cell(packed_ref, h, a, (b + db) % 4, c)
            return mid.at[h, da - 1, (b + db) % 4, c]

        far = []
        near = []
        for j, way in enumerate(ways):
            first = remote(held(2, core_for(j)), turn_last.at[h, j, da], place(h, 0, way, 0))
            second = remote(
                turn_last.at[h, j, da], cell(recv_ref, h, origin, (b - way) % 4, core),
                place(h, 0, way, j))
            far.append((first, second))
        for way in ways:
            for dc in range(2):
                near.append(remote(
                    held(way, core_for(dc)), cell(recv_ref, h, origin, b, core),
                    place(h, 0, way, dc)))
        near.append(remote(
            held(0, core_for(1)), cell(recv_ref, h, origin, b, core), place(h, 0, 0, 1)))
        own = pltpu.make_async_copy(
            held(0, core), cell(recv_ref, h, origin, b, core), own_sem.at[h, da])
        return far, near, own

    second_stage = {(h, da): last(h, da) for da in range(4) for h in halves}
    own_table = pltpu.make_async_copy(lengths_ref, table_ref.at[dev], own_sem.at[2, 0])
    own_table.start()
    pl.semaphore_wait(barrier, slots - 1)

    for copy in far_first.values():
        copy.start()
    for copy in near_first.values():
        copy.start()

    def send_table(k, carry):
        table_copy(k).start()
        return carry

    lax.fori_loop(1, slots, send_table, 0)

    def begin(h, da):
        far, near, own = second_stage[h, da]
        for first, _ in far:
            first.start()
        for copy in near:
            copy.start()
        own.start()

    def forward(h, da):
        for first, second in second_stage[h, da][0]:
            first.wait_recv()
            second.start()

    for key, copy in far_first.items():
        copy.wait_recv()
        far_second[key].start()
    for h in halves:
        begin(h, 0)
    for j, way in enumerate(ways):
        for h in halves:
            near_first[h, j].wait_recv()
            begin(h, 4 - way)
    for h in halves:
        forward(h, 0)
    for h in halves:
        for j in range(2):
            far_second[h, j].wait_recv()
        begin(h, 2)
    for da in (3, 1, 2):
        for h in halves:
            forward(h, da)
    for h in halves:
        for da in range(4):
            far, near, own = second_stage[h, da]
            for _, second in far:
                second.wait_recv()
            for copy in near:
                copy.wait_recv()
            own.wait()
    for copy in used:
        copy.wait_send()
    own_table.wait()

    def finish(k, carry):
        table_copy(k).wait()
        return carry

    lax.fori_loop(1, slots, finish, 0)


def exchange(counts, packed):
    slots, slot, width = packed.shape
    half = slot // 2
    kind = packed.dtype
    lengths = jnp.broadcast_to(jnp.pad(counts, (0, 128 - slots)), (8, 128))
    shape = (4, 4, 2, 2, half, width)
    copies = 12 + 8 * 9
    received, table = pl.pallas_call(
        exchange_kernel,
        out_shape=(
            jax.ShapeDtypeStruct(shape, kind),
            jax.ShapeDtypeStruct((slots, 8, 128), jnp.int32),
        ),
        in_specs=[
            pl.BlockSpec(memory_space=pltpu.VMEM),
            pl.BlockSpec(memory_space=pl.ANY),
        ],
        out_specs=(pl.BlockSpec(memory_space=pl.ANY), pl.BlockSpec(memory_space=pl.ANY)),
        scratch_shapes=[
            pltpu.VMEM((2, 3, 4, 2, half, width), kind),
            pltpu.VMEM((2, 2, 4, half, width), kind),
            pltpu.VMEM((2, 2, 4, half, width), kind),
            pltpu.SemaphoreType.DMA((slots,)),
            pltpu.SemaphoreType.DMA((slots,)),
            pltpu.SemaphoreType.DMA((copies,)),
            pltpu.SemaphoreType.DMA((copies,)),
            pltpu.SemaphoreType.DMA((3, 4)),
        ],
        compiler_params=pltpu.CompilerParams(collective_id=1, has_side_effects=True),
        name="ring_exchange",
    )(lengths, packed.reshape(shape))
    return received.reshape(slots, slot, width), table


def unpack_kernel(per_step, counts_ref, recv_ref, sensor_ref, power_ref, rows_ref):
    step = pl.program_id(0)
    slot = recv_ref.shape[1]
    owned = power_ref.shape[0]

    def skip(s, total):
        return total + counts_ref[s]

    at = lax.fori_loop(0, step * per_step, skip, jnp.int32(0))
    for i in range(per_step):
        for j in range(2):
            half = recv_ref[i, :, j * NU:(j + 1) * NU]
            rows_ref[j, pl.ds(at, slot), :] = half.astype(jnp.float32)
        at = at + counts_ref[step * per_step + i]

    @pl.when(step == pl.num_programs(0) - 1)
    def _():
        def tile(k, carry):
            here = pl.multiple_of(k * 128, 128)
            power_ref[pl.ds(here, 128), :] = rows_ref[0, pl.ds(here, 128), :].astype(power_ref.dtype)
            block = rows_ref[1, pl.ds(here, 128), :]
            sensor_ref[:, pl.ds(here, 128)] = block.T.astype(sensor_ref.dtype)
            return carry

        lax.fori_loop(0, owned // 128, tile, 0)


def unpack(counts, recv, owned):
    per_step = 4
    slots, slot, width = recv.shape
    return pl.pallas_call(
        functools.partial(unpack_kernel, per_step),
        out_shape=(
            jax.ShapeDtypeStruct((NU, owned), recv.dtype),
            jax.ShapeDtypeStruct((owned, NU), recv.dtype),
        ),
        grid_spec=pltpu.PrefetchScalarGridSpec(
            num_scalar_prefetch=1,
            grid=(slots // per_step,),
            in_specs=[pl.BlockSpec((per_step, slot, width), lambda i, c: (i, 0, 0))],
            out_specs=(
                pl.BlockSpec((NU, owned), lambda i, c: (0, 0)),
                pl.BlockSpec((owned, NU), lambda i, c: (0, 0)),
            ),
            scratch_shapes=[pltpu.VMEM((2, owned + slot, NU), jnp.float32)],
        ),
        name="unpack_rows",
    )(counts, recv)


def corr_kernel(scale, sensor_ref, power_ref, out_ref, *scratch):
    (wide, landed, rows, shifted, head, ex_send, ex_recv, edge_send, edge_recv,
     rs_send, rs_recv, first_recv) = scratch[:12]
    acc = scratch[12:18]
    got = scratch[18:24]
    owned = power_ref.shape[0]
    total = 2 * owned
    grp = lax.axis_index("grp")
    dev = lax.axis_index("dev")
    core = dev % 2
    chip = dev // 2
    y = chip % 4
    x = chip // 4
    partner = (grp, dev + 1 - 2 * core)
    after = (chip + 1) % 16
    before = (chip + 15) % 16

    def place(xx, yy, zz):
        return (zz, xx * 8 + yy * 2 + core)

    def near(a):
        return a + 1 - 2 * (a % 2)

    def far(a):
        return 3 - a

    neighbours = (
        place(near(x), y, grp), place(x, near(y), grp), place(x, y, near(grp)),
        place(far(x), y, grp), place(x, far(y), grp), place(x, y, far(grp)),
    )

    def near_bit(a):
        return (a // 2 + a % 2) % 2

    own_bits = (near_bit(x), near_bit(y), near_bit(grp), x // 2, y // 2, grp // 2)

    barrier = pltpu.get_barrier_semaphore()

    def greet(target):
        pl.semaphore_signal(barrier, inc=1, device_id=target, device_id_type=MESH)

    greet(partner)
    for target in neighbours:
        greet(target)
    greet((grp, before * 2 + 1))
    greet((grp, after * 2))
    greet((grp, jnp.where(core == 1, after * 2 + 1, before * 2)))
    pl.semaphore_wait(barrier, 10)

    own_at = pl.multiple_of(core * owned, 128)
    here = (
        (sensor_ref, wide.at[0:NU, pl.ds(own_at, owned)]),
        (power_ref, landed.at[pl.ds(pl.multiple_of(HALO + core * owned, 128), owned), :]),
    )
    exchange = [
        pltpu.make_async_remote_copy(
            src_ref=src, dst_ref=dst, send_sem=ex_send.at[i], recv_sem=ex_recv.at[i],
            device_id=partner, device_id_type=MESH)
        for i, (src, dst) in enumerate(here)
    ]
    edges = (
        (sensor_ref.at[:, 0:128], head, before),
        (power_ref.at[pl.ds(owned - HALO, HALO), :], landed.at[0:HALO, :], after),
    )

    def edge_copy(i, which):
        src, dst, target = edges[i]
        return pltpu.make_async_remote_copy(
            src_ref=src, dst_ref=dst, send_sem=edge_send.at[which], recv_sem=edge_recv.at[i],
            device_id=(grp, target * 2 + which), device_id_type=MESH)

    for i in range(2):
        @pl.when(core == i)
        def _(i=i):
            for which in range(2):
                edge_copy(i, which).start()

    for copy in exchange:
        copy.start()
    wide[0:NU, pl.ds(own_at, owned)] = sensor_ref[...]
    power_at = pl.multiple_of(HALO + core * owned, 128)
    rows[pl.ds(power_at, owned), :] = power_ref[...].astype(jnp.float32)
    exchange[1].wait_recv()
    other_at = pl.multiple_of(HALO + (1 - core) * owned, 128)
    rows[pl.ds(other_at, owned), :] = landed[pl.ds(other_at, owned), :].astype(jnp.float32)
    edge_copy(1, 0).wait_recv()
    rows[0:HALO, :] = jnp.where(chip > 0, landed[0:HALO, :].astype(jnp.float32), 0.0)

    def shift_rows(k, carry):
        at = pl.multiple_of(k * 912, 16)
        for u in range(4):
            shifted[u, pl.ds(at, 912), :] = rows[
                pl.ds(at + 16 - 4 * u - 2 * core, 912), :].astype(shifted.dtype)
        return carry

    lax.fori_loop(0, (LEAD + total) // 912, shift_rows, 0)

    edge_copy(0, 0).wait_recv()
    exchange[0].wait_recv()
    lane = lax.broadcasted_iota(jnp.int32, (NU, 128), 1)

    def turn(block):
        return pltpu.roll(block.astype(jnp.float32), 127, 1)

    def shift_lanes(k, following):
        at = pl.multiple_of(total - 128 - k * 128, 128)
        turned = turn(wide[0:NU, pl.ds(at, 128)])
        wide[NU:2 * NU, pl.ds(at, 128)] = jnp.where(lane == 127, following, turned).astype(wide.dtype)
        return turned

    lax.fori_loop(0, total // 128, shift_lanes, jnp.where(chip < 15, turn(head[...]), 0.0))

    def step_copy(step, q, src, dst):
        return pltpu.make_async_remote_copy(
            src_ref=src, dst_ref=dst, send_sem=rs_send.at[step, q], recv_sem=rs_recv.at[step, q],
            device_id=neighbours[(q + step) % DIMS], device_id_type=MESH)

    def read_at(bits):
        flip = [(o + b) % 2 for o, b in zip(own_bits, bits)]
        xd, yd, zd = (2 * flip[3 + i] + (flip[i] + flip[3 + i]) % 2 for i in range(3))
        return yd, pl.multiple_of(LEAD - 16 * (zd * 4 + xd), 16)

    def first_copy(q, index):
        slot = index % (BLOCKS // 2)
        return pltpu.make_async_remote_copy(
            src_ref=acc[q].at[slot + BLOCKS // 2], dst_ref=got[q].at[slot],
            send_sem=rs_send.at[0, q], recv_sem=first_recv.at[q, slot],
            device_id=neighbours[q], device_id_type=MESH)

    def bits_of(i):
        first = BLOCKS - 1 - 2 * i
        return [
            [1 - j] + [(first // 2 ** b) % 2 for b in range(1, DIMS)] for j in range(2)]

    def index_of(q, bits):
        return sum(bits[(q + e) % DIMS] * 2 ** (DIMS - 1 - e) for e in range(DIMS))

    def follow(i):
        both = bits_of(i)

        def take(q, j):
            index = index_of(q, both[j]) % (BLOCKS // 2)
            first_copy(q, index).wait_recv()
            acc[q][index] = acc[q][index] + got[q][index]
            return index

        def pass_on(q, index):
            low = index % (BLOCKS // 4)
            step_copy(
                1, q, acc[q].at[low + BLOCKS // 4], got[q].at[low + BLOCKS // 2]).start()

        for q in range(DIMS):
            which = (1,) if q == 0 else (0, 1)

            def step(q=q, which=which):
                taken = [take(q, j) for j in which]
                if q == DIMS - 1:
                    pass_on(q, taken[0])
                else:
                    @pl.when(both[0][q + 1] == 1)
                    def _():
                        for index in taken:
                            pass_on(q, index)

            if q == 0:
                step()
            else:
                pl.when(both[0][q] == 0)(step)

    def pair(i, carry):
        both = bits_of(i)
        reads = [read_at(bits) for bits in both]
        result = None
        for k in range(0, total, K_CHUNK):
            operand = jnp.concatenate(
                [shifted[u, pl.ds(at + k, K_CHUNK), :] for u, at in reads], axis=1)
            term = jnp.dot(wide[:, k:k + K_CHUNK], operand, preferred_element_type=jnp.float32)
            result = term if result is None else result + term
        for q in range(DIMS):
            for j in range(2):
                acc[q][index_of(q, both[j])] = result[
                    PART_AT[q]:PART_AT[q] + PARTS[q], j * NU:(j + 1) * NU]
            if q == 0:
                first_copy(q, index_of(q, both[0])).start()
            else:
                @pl.when(both[0][q] == 1)
                def _(q=q):
                    for j in range(2):
                        first_copy(q, index_of(q, both[j])).start()

        @pl.when(i >= BEHIND)
        def _():
            follow(i - BEHIND)

        return carry

    lax.fori_loop(0, BLOCKS // 2, pair, 0)

    def rest(i, carry):
        follow(i)
        return carry

    lax.fori_loop(BLOCKS // 2 - BEHIND, BLOCKS // 2, rest, 0)

    sent = [
        [step_copy(0, q, acc[q].at[32:64], got[q].at[0:32]) for q in range(DIMS)],
        [step_copy(1, q, acc[q].at[16:32], got[q].at[32:48]) for q in range(DIMS)],
    ]
    begin = BLOCKS // 2
    for step in range(2, DIMS):
        n = 2 ** (DIMS - 1 - step)
        copies = []
        for q in range(DIMS):
            sent[step - 1][q].wait_recv()
            acc[q][n:2 * n] = acc[q][n:2 * n] + got[q][begin + n:begin + 2 * n]
            copy = step_copy(
                step, q, acc[q].at[n:2 * n], got[q].at[begin + 2 * n:begin + 3 * n])
            copy.start()
            copies.append(copy)
        for q in range(DIMS):
            acc[q][0:n] = acc[q][0:n] + got[q][begin:begin + n]
        sent.append(copies)
        begin += 2 * n
    for q in range(DIMS):
        sent[DIMS - 1][q].wait_recv()
        out_ref[PART_AT[q]:PART_AT[q] + PARTS[q], :] = (acc[q][0] + got[q][begin]) * scale

    for copies in sent:
        for copy in copies:
            copy.wait_send()
    for copy in exchange:
        copy.wait_send()

    for i in range(2):
        @pl.when(core == i)
        def _(i=i):
            for which in range(2):
                edge_copy(i, which).wait_send()


def correlate(sensor, power, scale):
    owned = power.shape[0]
    total = 2 * owned
    kind = power.dtype
    return pl.pallas_call(
        functools.partial(corr_kernel, scale),
        out_shape=jax.ShapeDtypeStruct((2 * NU, NU), jnp.float32),
        in_specs=[pl.BlockSpec(memory_space=pltpu.VMEM)] * 2,
        out_specs=pl.BlockSpec(memory_space=pltpu.VMEM),
        scratch_shapes=[
            pltpu.VMEM((2 * NU, total), kind),
            pltpu.VMEM((HALO + total, NU), kind),
            pltpu.VMEM((HALO + total, NU), jnp.float32),
            pltpu.VMEM((4, LEAD + total, NU), kind),
            pltpu.VMEM((NU, 128), kind),
            pltpu.SemaphoreType.DMA((2,)),
            pltpu.SemaphoreType.DMA((2,)),
            pltpu.SemaphoreType.DMA((2,)),
            pltpu.SemaphoreType.DMA((2,)),
            pltpu.SemaphoreType.DMA((DIMS, DIMS)),
            pltpu.SemaphoreType.DMA((DIMS, DIMS)),
            pltpu.SemaphoreType.DMA((DIMS, BLOCKS // 2)),
        ]
        + [pltpu.VMEM((BLOCKS, h, NU), jnp.float32) for h in PARTS]
        + [pltpu.VMEM((BLOCKS - 1, h, NU), jnp.float32) for h in PARTS],
        compiler_params=pltpu.CompilerParams(
            collective_id=0, has_side_effects=True, vmem_limit_bytes=56 << 20),
        name="correlate_scatter",
    )(sensor, power)


def per_device(trace, counts):
    dev_count = lax.axis_size("dev")
    group_count = lax.axis_size("grp")
    capacity = trace.shape[0]
    slot_rows = capacity // dev_count
    owned = capacity // 2
    send_counts = counts.reshape(-1)
    received, table = exchange(send_counts, pack(send_counts, trace, dev_count, slot_rows))
    recv_counts = lax.dynamic_index_in_dim(table[:, 0, :], lax.axis_index("dev"), 1, False)
    sensor, power = unpack(recv_counts, received, owned)
    scale = 1.0 / math.sqrt(group_count * dev_count * owned)
    return correlate(sensor, power, scale).reshape(2, NU, NU)


def solution(mesh):
    in_specs = (P(("grp", "dev"), None), P("grp", "dev", None))
    out_specs = P(("grp", "dev"), None, None)
    return jax.shard_map(
        per_device, mesh=mesh, in_specs=in_specs, out_specs=out_specs, check_vma=False
    )
```
